32 devices in a mesh: gz: 8 (over z, x), gy: 4 (over y, core).
Axes of the slice: x: 2, y: 2, z: 4, core: 2. Of those that a mesh axis runs over, the one named last changes fastest.
Arguments:
- volume: bfloat16 [32, 16, 32, 128], P('gz', 'gy'), may hold values from -6 to 6
- kernel_a: bfloat16 [3, 3, 3, 128, 128], replicated, may hold values from -0.109375 to 0.109375
- bias_a: float32 [128], replicated, may hold values from -3 to 3
- kernel_b: bfloat16 [3, 3, 3, 128, 256], P(None, None, None, None, 'gy'), may hold values from -0.109375 to 0.109375
- bias_b: float32 [256], P('gy'), may hold values from -3 to 3
- kernel_c: bfloat16 [3, 3, 3, 256, 512], P(None, None, None, None, 'gy'), may hold values from -0.078125 to 0.078125
- bias_c: float32 [512], P('gy'), may hold values from -3 to 3
Outputs:
- skip_a: bfloat16 [32, 16, 32, 128], P('gz', 'gy')
- skip_b: bfloat16 [16, 8, 16, 256], P('gz', None, None, 'gy')
- bottom: bfloat16 [8, 4, 8, 512], P('gz', None, None, 'gy')
The draws below stay inside these ranges and needn't reach their ends.
All inputs are finite; a program needn't handle non-finite values.
Results may differ from the reference program's by a relative error of at most 0.0054.
Values may be sent and summed in bfloat16 or wider, within the bound.
A program may use at most 64 MiB of HBM per device.

```python
import jax
import jax.numpy as jnp
from jax import lax

CA = 128
CB = 256
CC = 512
XW = 32
DA = 32
HA = 16


def block_scale(key, dims, shards, least, largest):
    def one(position, parts):
        heights = jax.random.uniform(jax.random.fold_in(jax.random.fold_in(key, 6), position), (parts,), jnp.float32, least / len(shards), largest / len(shards))
        return jnp.repeat(jnp.exp(heights), dims[position] // parts).reshape((-1,) + (1,) * (len(dims) - position - 1))

    loudness = one(*shards[0])
    for cut in shards[1:]:
        loudness = loudness * one(*cut)
    return loudness


def normal_values(rng, dims, scale, most, cuts=(), dtype=jnp.bfloat16):
    entries = jax.random.normal(rng, dims, jnp.float32) * scale
    if len(cuts) > 0:
        entries = block_scale(rng, dims, cuts, -0.22, 0.18) * entries
    return jnp.clip(entries, min=-most, max=most).astype(dtype)


def setup_inputs(seed: int = 0) -> dict:
    key_of = jax.random.split(jax.random.key(seed), 8)
    return {
        "volume": normal_values(key_of[0], (DA, HA, XW, CA), 1.0, 6.0, ((0, 8), (1, 4))),
        "kernel_a": normal_values(key_of[1], (3, 3, 3, CA, CA), (27 * CA) ** -0.5, 0.109375),
        "bias_a": normal_values(key_of[2], (CA,), 0.5, 3.0, (), jnp.float32),
        "kernel_b": normal_values(key_of[3], (3, 3, 3, CA, CB), (27 * CA) ** -0.5, 0.109375, ((4, 4),)),
        "bias_b": normal_values(key_of[4], (CB,), 0.5, 3.0, ((0, 4),), jnp.float32),
        "kernel_c": normal_values(key_of[5], (3, 3, 3, CB, CC), (27 * CB) ** -0.5, 0.078125, ((4, 4),)),
        "bias_c": normal_values(key_of[6], (CC,), 0.5, 3.0, ((0, 4),), jnp.float32),
    }


def conv_relu(field, kernel, bias):
    out = lax.conv_general_dilated(field[None], kernel, (1, 1, 1), ((1, 1), (1, 1), (1, 1)), dimension_numbers=("NDHWC", "DHWIO", "NDHWC"), preferred_element_type=jnp.float32)[0]
    return jnp.maximum(out + bias.astype(jnp.float32), 0.0).astype(jnp.bfloat16)


def shrink(field):
    depth, height, width, chans = field.shape
    blocks = field.reshape(depth // 2, 2, height // 2, 2, width // 2, 2, chans)
    return jnp.max(blocks, axis=(1, 3, 5))


def reference(volume, kernel_a, bias_a, kernel_b, bias_b, kernel_c, bias_c):
    skip_a = conv_relu(volume, kernel_a, bias_a)
    skip_b = conv_relu(shrink(skip_a), kernel_b, bias_b)
    bottom = conv_relu(shrink(skip_b), kernel_c, bias_c)
    return skip_a, skip_b, bottom
```

```python
import functools

import jax
import jax.numpy as jnp
from jax import lax
from jax.experimental import pallas as pl
from jax.experimental.pallas import tpu as pltpu
from jax.sharding import PartitionSpec as P

F32 = jnp.float32
BF16 = jnp.bfloat16
MESH = pl.DeviceIdType.MESH


def tapped(rows, width):
    count = rows.shape[0]
    x = lax.broadcasted_iota(jnp.int32, rows.shape, 0) % width
    left = jnp.where(x == 0, 0.0, pltpu.roll(rows, 1, 0))
    right = jnp.where(x == width - 1, 0.0, pltpu.roll(rows, count - 1, 0))
    return jnp.concatenate([left, rows, right], axis=-1)


def dot(a, b):
    return jnp.dot(a, b, preferred_element_type=F32)


def kernel(
    n_z, n_y,
    vol, ka, ba, kb, bb, kc, bc,
    out_a, out_b, out_c,
    loc, hz, hy, wa, wb, wc,
    sa, sz, sy, acc_a, pool_a, ga, sb, acc_b, pool_b, gb, sc,
    load_sem, hs_sem, hr_sem, as_sem, ar_sem, bs_sem, br_sem,
):
    z = lax.axis_index("gz")
    y = lax.axis_index("gy")
    d, h, xw, ca = vol.shape
    d2, h2, x2 = d // 2, h // 2, xw // 2
    hh = h2 * n_y
    cb = kb.shape[-1]
    h4, x4 = hh // 2, x2 // 2
    lanes = gb.shape[-1]
    per = lanes // cb

    loads = [
        pltpu.make_async_copy(vol, loc, load_sem.at[0]),
        pltpu.make_async_copy(ka, wa, load_sem.at[1]),
        pltpu.make_async_copy(kb, wb, load_sem.at[2]),
        pltpu.make_async_copy(kc, wc, load_sem.at[3]),
    ]
    for load in loads:
        load.start()

    has_lo, has_hi = z > 0, z < n_z - 1

    barrier = pltpu.get_barrier_semaphore()
    for away, has in ((-1, has_lo), (1, has_hi)):
        @pl.when(has)
        def _():
            for k in range(n_y):
                pl.semaphore_signal(barrier, inc=1, device_id=(z + away, k), device_id_type=MESH)
    for k in range(1, n_y):
        pl.semaphore_signal(barrier, inc=1, device_id=(z, lax.rem(y + k, n_y)), device_id_type=MESH)
    sides = jnp.where(has_lo, 1, 0) + jnp.where(has_hi, 1, 0)

    def halo(index, dz, dy):
        layer = d - 1 if dz > 0 else 0
        row = h - 1 if dy > 0 else 0
        slot = 0 if dz > 0 else 1
        if dz == 0:
            src, dst = vol.at[:, row], hy.at[0 if dy > 0 else 1]
        elif dy == 0:
            src, dst = vol.at[layer], hz.at[slot, pl.ds(1, h)]
        else:
            src, dst = vol.at[layer, row], hz.at[slot, 0 if dy > 0 else h + 1]
        return pltpu.make_async_remote_copy(
            src_ref=src, dst_ref=dst, send_sem=hs_sem.at[index], recv_sem=hr_sem.at[index],
            device_id=(z + dz, y + dy), device_id_type=MESH,
        )

    def inside(dz, dy):
        ok = None
        for pos, count, step in ((z, n_z, dz), (y, n_y, dy)):
            if step:
                one = pos > 0 if step < 0 else pos < count - 1
                ok = one if ok is None else jnp.logical_and(ok, one)
        return ok

    moves = [(-1, 0), (1, 0), (-1, -1), (-1, 1), (1, -1), (1, 1), (0, -1), (0, 1)]
    pl.semaphore_wait(barrier, sides * n_y + n_y - 1)
    for index, (dz, dy) in enumerate(moves):
        @pl.when(inside(dz, dy))
        def _():
            halo(index, dz, dy).start()

    for slot, has in ((0, has_lo), (1, has_hi)):
        @pl.when(jnp.logical_not(has))
        def _():
            hz[slot] = jnp.zeros(hz.shape[1:], BF16)
            ga[slot * (d2 + 1)] = jnp.zeros(ga.shape[1:], BF16)
            gb[slot * 2] = jnp.zeros(gb.shape[1:], BF16)
    for slot, has_y, row in ((0, y > 0, 0), (1, y < n_y - 1, h + 1)):
        @pl.when(jnp.logical_not(has_y))
        def _():
            hy[slot] = jnp.zeros(hy.shape[1:], BF16)
            for s, has in ((0, has_lo), (1, has_hi)):
                @pl.when(has)
                def _():
                    hz[s, row] = jnp.zeros(hz.shape[2:], BF16)
    for row in (0, hh + 1):
        sb[:, row] = jnp.zeros((d2 + 2,) + sb.shape[2:], BF16)
    for row in (0, h4 + 1):
        sc[:, row] = jnp.zeros((3,) + sc.shape[2:], F32)
    for slot in (0, 1):
        for end in (0, d + 1):
            sy[slot, end] = jnp.zeros(sy.shape[2:], BF16)

    loads[0].wait()
    sa[...] = tapped(loc[...].astype(F32).reshape(d * h * xw, ca), xw).astype(BF16).reshape(sa.shape)
    loads[1].wait()
    k3 = 3 * ca

    def span(tap, count):
        low, high = max(0, 1 - tap), min(count, count + 1 - tap)
        return low, high, low + tap - 1, high + tap - 1

    bias = jnp.broadcast_to(ba[...], (d * h * xw, ca)).reshape(d, h, xw, ca)
    acc_a[...] = bias + dot(sa[...].reshape(d * h * xw, k3), wa[1, 1]).reshape(d, h, xw, ca)
    for i in range(3):
        for j in range(3):
            if (i, j) == (1, 1):
                continue
            z0, z1, f0, f1 = span(i, d)
            y0, y1, g0, g1 = span(j, h)
            rows = sa[f0:f1, g0:g1].reshape(-1, k3)
            acc_a[z0:z1, y0:y1] += dot(rows, wa[i, j]).reshape(z1 - z0, y1 - y0, xw, ca)

    for index, (dz, dy) in enumerate(moves):
        if dz == 0:
            @pl.when(inside(-dz, -dy))
            def _():
                halo(index, dz, dy).wait_recv()
    for slot, row, tap in ((0, 0, 0), (1, h - 1, 2)):
        sy[slot, 1:d + 1] = tapped(hy[slot].astype(F32).reshape(d * xw, ca), xw).astype(BF16).reshape(d, xw, k3)
        total = acc_a[:, row].reshape(d * xw, ca)
        for i in range(3):
            total += dot(sy[slot, i:i + d].reshape(d * xw, k3), wa[i, tap])
        acc_a[:, row] = total.reshape(d, xw, ca)
    for index, (dz, dy) in enumerate(moves):
        if dz != 0:
            @pl.when(inside(-dz, -dy))
            def _():
                halo(index, dz, dy).wait_recv()
    for slot, layer, tap in ((0, 0, 0), (1, d - 1, 2)):
        sz[slot] = tapped(hz[slot].astype(F32).reshape((h + 2) * xw, ca), xw).astype(BF16).reshape(h + 2, xw, k3)
        total = acc_a[layer].reshape(h * xw, ca)
        for j in range(3):
            total += dot(sz[slot, j:j + h].reshape(h * xw, k3), wa[tap, j])
        acc_a[layer] = total.reshape(h, xw, ca)

    full = jnp.maximum(acc_a[...], 0.0)
    paired = jnp.max(full.reshape(d2, 2, h2, 2, xw, ca), axis=(1, 3))
    pool_a[...] = paired.reshape(d2 * h2 * xw, ca)
    half = d2 * h2 * x2
    small = jnp.maximum(pool_a[pl.ds(0, half, stride=2)], pool_a[pl.ds(1, half, stride=2)])
    mine = pl.ds(y * h2, h2)
    ga[1:d2 + 1, mine] = small.astype(BF16).reshape(d2, h2, x2, ca)

    def send_lower(buf, edge_lo, edge_hi, own_layers, top, row_slice, s_sem, r_sem):
        def to_side(slot, k):
            src = buf.at[edge_lo if slot == 0 else edge_hi, row_slice]
            dst = buf.at[top if slot == 0 else 0, row_slice]
            return pltpu.make_async_remote_copy(
                src_ref=src, dst_ref=dst, send_sem=s_sem.at[slot, k], recv_sem=r_sem.at[slot, y],
                device_id=(z + (2 * slot - 1), k), device_id_type=MESH,
            )

        def to_peer(k):
            part = buf.at[own_layers, row_slice]
            return pltpu.make_async_remote_copy(
                src_ref=part, dst_ref=part, send_sem=s_sem.at[2, k], recv_sem=r_sem.at[2, y],
                device_id=(z, lax.rem(y + k, n_y)), device_id_type=MESH,
            )

        return to_side, to_peer

    def start_all(to_side, to_peer):
        for slot, has in ((0, has_lo), (1, has_hi)):
            @pl.when(has)
            def _():
                for k in range(n_y):
                    to_side(slot, k).start()
        for k in range(1, n_y):
            to_peer(k).start()

    def await_sends(to_side, to_peer):
        for slot, has in ((0, has_lo), (1, has_hi)):
            @pl.when(has)
            def _():
                for k in range(n_y):
                    to_side(slot, k).wait_send()
        for k in range(1, n_y):
            to_peer(k).wait_send()

    def recv(dst, sem, s_sem):
        pltpu.make_async_remote_copy(
            src_ref=dst, dst_ref=dst, send_sem=s_sem, recv_sem=sem, device_id=(z, y), device_id_type=MESH
        ).wait_recv()

    side_a, peer_a = send_lower(ga, 1, d2, pl.ds(1, d2), d2 + 1, mine, as_sem, ar_sem)
    start_all(side_a, peer_a)
    out_a[...] = full.astype(BF16)

    def tapped_b(first, count):
        rows = ga[first:first + count].astype(F32).reshape(count * hh * x2, ca)
        sb[first:first + count, 1:hh + 1] = tapped(rows, x2).astype(BF16).reshape(count, hh, x2, k3)

    def part_b(first, count, i):
        rows = jnp.concatenate([sb[first:first + count, j:j + hh].reshape(count * hh * x2, k3) for j in range(3)], axis=-1)
        return dot(rows, wb[i]).reshape(count, hh, x2, cb)

    loads[2].wait()
    for k in range(1, n_y):
        q = lax.rem(y + k, n_y)
        recv(ga.at[pl.ds(1, d2), pl.ds(q * h2, h2)], ar_sem.at[2, q], as_sem.at[2, k])
    tapped_b(1, d2)
    bias = jnp.broadcast_to(bb[...], (d2 * hh * x2, cb)).reshape(d2, hh, x2, cb)
    acc_b[...] = bias + part_b(1, d2, 1)
    acc_b[1:] += part_b(1, d2 - 1, 0)
    acc_b[:d2 - 1] += part_b(2, d2 - 1, 2)
    for slot, has, first, layer, i in ((1, has_lo, 0, 0, 0), (0, has_hi, d2 + 1, d2 - 1, 2)):
        @pl.when(has)
        def _():
            for k in range(n_y):
                recv(ga.at[first, pl.ds(k * h2, h2)], ar_sem.at[slot, k], as_sem.at[slot, k])
        tapped_b(first, 1)
        acc_b[layer] += part_b(first, 1, i)[0]

    full_b = jnp.maximum(acc_b[...], 0.0)
    paired = jnp.max(full_b.reshape(hh // 2, 2, x2, cb) if d2 == 1 else jnp.max(full_b, axis=0).reshape(h4, 2, x2, cb), axis=1)
    wide = []
    for q in range(per):
        parts = [jnp.where(lax.rem(y, per) == q, paired, 0.0) if p == q else jnp.zeros_like(paired) for p in range(per)]
        wide.append(jnp.concatenate(parts, axis=-1))
    pool_b[...] = functools.reduce(jnp.add, wide).reshape(h4 * x2, lanes)
    small = jnp.maximum(pool_b[pl.ds(0, h4 * x4, stride=2)], pool_b[pl.ds(1, h4 * x4, stride=2)])
    gb[1, pl.ds(y, 1)] = small.astype(BF16)[None]
    side_b, peer_b = send_lower(gb, 1, 1, 1, 2, pl.ds(y, 1), bs_sem, br_sem)
    start_all(side_b, peer_b)
    out_b[...] = full_b.astype(BF16)

    cells = h4 * x4

    def part_c(layer):
        groups = []
        for g in range(n_y // per):
            groups.append(functools.reduce(jnp.add, [gb[layer, g * per + p].astype(F32) for p in range(per)]))
        rows = jnp.concatenate(groups, axis=-1)
        sc[layer, 1:h4 + 1] = tapped(rows, x4).reshape(h4, x4, sc.shape[-1])
        lhs = jnp.concatenate([sc[layer, j:j + h4].reshape(cells, sc.shape[-1]) for j in range(3)], axis=-1)
        return dot(lhs.astype(BF16), wc[layer])

    loads[3].wait()
    for k in range(1, n_y):
        q = lax.rem(y + k, n_y)
        recv(gb.at[1, pl.ds(q, 1)], br_sem.at[2, q], bs_sem.at[2, k])
    total = bc[...] + part_c(1)
    for slot, has, layer in ((1, has_lo, 0), (0, has_hi, 2)):
        @pl.when(has)
        def _():
            for k in range(n_y):
                recv(gb.at[layer, pl.ds(k, 1)], br_sem.at[slot, k], bs_sem.at[slot, k])
    total += part_c(0) + part_c(2)
    out_c[...] = jnp.maximum(total, 0.0).astype(BF16)

    for index, (dz, dy) in enumerate(moves):
        @pl.when(inside(dz, dy))
        def _():
            halo(index, dz, dy).wait_send()
    await_sends(side_a, peer_a)
    await_sends(side_b, peer_b)


def on_device(n_z, n_y, volume, kernel_a, bias_a, kernel_b, bias_b, kernel_c, bias_c):
    d, h, xw, ca = volume.shape
    cb, cc = kernel_b.shape[-1], kernel_c.shape[-1]
    c_in = kernel_c.shape[-2]
    d2, h2, x2 = d // 2, h // 2, xw // 2
    hh = h2 * n_y
    h4, x4 = hh // 2, x2 // 2
    lanes = 128
    wa = kernel_a.reshape(3, 3, 3 * ca, ca)
    wb = kernel_b.reshape(3, 9 * ca, cb)
    wc = kernel_c.reshape(3, 9 * c_in, cc)
    vmem = pl.BlockSpec(memory_space=pltpu.VMEM)
    hbm = pl.BlockSpec(memory_space=pl.ANY)
    out_a, out_b, out_c = pl.pallas_call(
        functools.partial(kernel, n_z, n_y),
        out_shape=(
            jax.ShapeDtypeStruct((d, h, xw, ca), BF16),
            jax.ShapeDtypeStruct((d2, hh, x2, cb), BF16),
            jax.ShapeDtypeStruct((h4 * x4, cc), BF16),
        ),
        in_specs=[hbm, hbm, vmem, hbm, vmem, hbm, vmem],
        out_specs=(vmem, vmem, vmem),
        scratch_shapes=[
            pltpu.VMEM(volume.shape, BF16),
            pltpu.VMEM((2, h + 2, xw, ca), BF16),
            pltpu.VMEM((2, d, xw, ca), BF16),
            pltpu.VMEM(wa.shape, BF16),
            pltpu.VMEM(wb.shape, BF16),
            pltpu.VMEM(wc.shape, BF16),
            pltpu.VMEM((d, h, xw, 3 * ca), BF16),
            pltpu.VMEM((2, h + 2, xw, 3 * ca), BF16),
            pltpu.VMEM((2, d + 2, xw, 3 * ca), BF16),
            pltpu.VMEM((d, h, xw, ca), F32),
            pltpu.VMEM((d2 * h2 * xw, ca), F32),
            pltpu.VMEM((d2 + 2, hh, x2, ca), BF16),
            pltpu.VMEM((d2 + 2, hh + 2, x2, 3 * ca), BF16),
            pltpu.VMEM((d2, hh, x2, cb), F32),
            pltpu.VMEM((h4 * x2, lanes), F32),
            pltpu.VMEM((3, n_y, h4 * x4, lanes), BF16),
            pltpu.VMEM((3, h4 + 2, x4, 3 * c_in), F32),
            pltpu.SemaphoreType.DMA((4,)),
            pltpu.SemaphoreType.DMA((8,)),
            pltpu.SemaphoreType.DMA((8,)),
            pltpu.SemaphoreType.DMA((3, n_y)),
            pltpu.SemaphoreType.DMA((3, n_y)),
            pltpu.SemaphoreType.DMA((3, n_y)),
            pltpu.SemaphoreType.DMA((3, n_y)),
        ],
        compiler_params=pltpu.CompilerParams(collective_id=0, has_side_effects=True),
        name="unet",
    )(volume, wa, bias_a.reshape(1, -1), wb, bias_b.reshape(1, -1), wc, bias_c.reshape(1, -1))
    return out_a, out_b, out_c.reshape(d2 // 2, h4, x4, cc)


def solution(mesh):
    sizes = dict(mesh.shape)
    return jax.shard_map(
        functools.partial(on_device, sizes["gz"], sizes["gy"]),
        mesh=mesh,
        in_specs=(
            P("gz", "gy", None, None),
            P(),
            P(),
            P(None, None, None, None, "gy"),
            P("gy"),
            P(None, None, None, None, "gy"),
            P("gy"),
        ),
        out_specs=(P("gz", "gy", None, None), P("gz", None, None, "gy"), P("gz", None, None, "gy")),
        check_vma=False,
    )
```

```python
import functools

import jax
import jax.numpy as jnp
from jax import lax
from jax.experimental import pallas as pl
from jax.experimental.pallas import tpu as pltpu
from jax.sharding import PartitionSpec as P

F32 = jnp.float32
BF16 = jnp.bfloat16
MESH = pl.DeviceIdType.MESH


def tapped(rows, width):
    count = rows.shape[0]
    x = lax.broadcasted_iota(jnp.int32, rows.shape, 0) % width
    left = jnp.where(x == 0, 0.0, pltpu.roll(rows, 1, 0))
    right = jnp.where(x == width - 1, 0.0, pltpu.roll(rows, count - 1, 0))
    return jnp.concatenate([left, rows, right], axis=-1)


def dot(a, b):
    return jnp.dot(a, b, preferred_element_type=F32)


def kernel(
    n_z, n_y,
    vol, ka, ba, kb, bb, kc, bc,
    out_a, out_b, out_c,
    loc, hz, hy, wa, wt, wb, wc,
    sa, sz, sy, acc_a, pool_a, ga, sb, acc_b, pool_b, gb, sc,
    load_sem, hs_sem, hr_sem, as_sem, ar_sem, bs_sem, br_sem,
):
    z = lax.axis_index("gz")
    y = lax.axis_index("gy")
    d, h, xw, ca = vol.shape
    d2, h2, x2 = d // 2, h // 2, xw // 2
    hh = h2 * n_y
    cb = kb.shape[-2]
    h4, x4 = hh // 2, x2 // 2
    lanes = gb.shape[-1]
    per = lanes // cb

    loads = [
        pltpu.make_async_copy(vol, loc, load_sem.at[0]),
        pltpu.make_async_copy(ka, wa, load_sem.at[1]),
        pltpu.make_async_copy(kb, wt, load_sem.at[2]),
        pltpu.make_async_copy(kc, wc, load_sem.at[3]),
    ]
    for load in loads:
        load.start()

    has_lo, has_hi = z > 0, z < n_z - 1

    barrier = pltpu.get_barrier_semaphore()
    for away, has in ((-1, has_lo), (1, has_hi)):
        @pl.when(has)
        def _():
            for k in range(n_y):
                pl.semaphore_signal(barrier, inc=1, device_id=(z + away, k), device_id_type=MESH)
    for k in range(1, n_y):
        pl.semaphore_signal(barrier, inc=1, device_id=(z, lax.rem(y + k, n_y)), device_id_type=MESH)
    sides = jnp.where(has_lo, 1, 0) + jnp.where(has_hi, 1, 0)

    def halo(index, dz, dy):
        layer = d - 1 if dz > 0 else 0
        row = h - 1 if dy > 0 else 0
        slot = 0 if dz > 0 else 1
        if dz == 0:
            src, dst = vol.at[:, row], hy.at[0 if dy > 0 else 1]
        elif dy == 0:
            src, dst = vol.at[layer], hz.at[slot, pl.ds(1, h)]
        else:
            src, dst = vol.at[layer, row], hz.at[slot, 0 if dy > 0 else h + 1]
        return pltpu.make_async_remote_copy(
            src_ref=src, dst_ref=dst, send_sem=hs_sem.at[index], recv_sem=hr_sem.at[index],
            device_id=(z + dz, y + dy), device_id_type=MESH,
        )

    def inside(dz, dy):
        ok = None
        for pos, count, step in ((z, n_z, dz), (y, n_y, dy)):
            if step:
                one = pos > 0 if step < 0 else pos < count - 1
                ok = one if ok is None else jnp.logical_and(ok, one)
        return ok

    moves = [(-1, 0), (1, 0), (-1, -1), (-1, 1), (1, -1), (1, 1), (0, -1), (0, 1)]
    pl.semaphore_wait(barrier, sides * n_y + n_y - 1)
    for index, (dz, dy) in enumerate(moves):
        @pl.when(inside(dz, dy))
        def _():
            halo(index, dz, dy).start()

    for slot, has in ((0, has_lo), (1, has_hi)):
        @pl.when(jnp.logical_not(has))
        def _():
            hz[slot] = jnp.zeros(hz.shape[1:], BF16)
            ga[slot * (d2 + 1)] = jnp.zeros(ga.shape[1:], BF16)
            gb[slot * 2] = jnp.zeros(gb.shape[1:], BF16)
    for slot, has_y, row in ((0, y > 0, 0), (1, y < n_y - 1, h + 1)):
        @pl.when(jnp.logical_not(has_y))
        def _():
            hy[slot] = jnp.zeros(hy.shape[1:], BF16)
            for s, has in ((0, has_lo), (1, has_hi)):
                @pl.when(has)
                def _():
                    hz[s, row] = jnp.zeros(hz.shape[2:], BF16)
    for row in (0, hh + 1):
        sb[:, row] = jnp.zeros((d2 + 2,) + sb.shape[2:], BF16)
    for row in (0, h4 + 1):
        sc[:, row] = jnp.zeros((3,) + sc.shape[2:], F32)
    for slot in (0, 1):
        for end in (0, d + 1):
            sy[slot, end] = jnp.zeros(sy.shape[2:], BF16)

    loads[0].wait()
    sa[...] = tapped(loc[...].astype(F32).reshape(d * h * xw, ca), xw).astype(BF16).reshape(sa.shape)
    loads[1].wait()
    k3 = 3 * ca

    def span(tap, count):
        low, high = max(0, 1 - tap), min(count, count + 1 - tap)
        return low, high, low + tap - 1, high + tap - 1

    bias = jnp.broadcast_to(ba[...], (d * h * xw, ca)).reshape(d, h, xw, ca)
    acc_a[...] = bias + dot(sa[...].reshape(d * h * xw, k3), wa[1, 1]).reshape(d, h, xw, ca)
    for i in range(3):
        for j in range(3):
            if (i, j) == (1, 1):
                continue
            z0, z1, f0, f1 = span(i, d)
            y0, y1, g0, g1 = span(j, h)
            rows = sa[f0:f1, g0:g1].reshape(-1, k3)
            acc_a[z0:z1, y0:y1] += dot(rows, wa[i, j]).reshape(z1 - z0, y1 - y0, xw, ca)

    for index, (dz, dy) in enumerate(moves):
        if dz == 0:
            @pl.when(inside(-dz, -dy))
            def _():
                halo(index, dz, dy).wait_recv()
    for slot, row, tap in ((0, 0, 0), (1, h - 1, 2)):
        sy[slot, 1:d + 1] = tapped(hy[slot].astype(F32).reshape(d * xw, ca), xw).astype(BF16).reshape(d, xw, k3)
        total = acc_a[:, row].reshape(d * xw, ca)
        for i in range(3):
            total += dot(sy[slot, i:i + d].reshape(d * xw, k3), wa[i, tap])
        acc_a[:, row] = total.reshape(d, xw, ca)
    for index, (dz, dy) in enumerate(moves):
        if dz != 0:
            @pl.when(inside(-dz, -dy))
            def _():
                halo(index, dz, dy).wait_recv()
    for slot, layer, tap in ((0, 0, 0), (1, d - 1, 2)):
        sz[slot] = tapped(hz[slot].astype(F32).reshape((h + 2) * xw, ca), xw).astype(BF16).reshape(h + 2, xw, k3)
        total = acc_a[layer].reshape(h * xw, ca)
        for j in range(3):
            total += dot(sz[slot, j:j + h].reshape(h * xw, k3), wa[tap, j])
        acc_a[layer] = total.reshape(h, xw, ca)

    full = jnp.maximum(acc_a[...], 0.0)
    paired = jnp.max(full.reshape(d2, 2, h2, 2, xw, ca), axis=(1, 3))
    pool_a[...] = paired.reshape(d2 * h2 * xw, ca)
    half = d2 * h2 * x2
    small = jnp.maximum(pool_a[pl.ds(0, half, stride=2)], pool_a[pl.ds(1, half, stride=2)])
    mine = pl.ds(y * h2, h2)
    ga[1:d2 + 1, mine] = small.astype(BF16).reshape(d2, h2, x2, ca)

    def send_lower(buf, edge_lo, edge_hi, own_layers, top, row_slice, s_sem, r_sem):
        def to_side(slot, k):
            src = buf.at[edge_lo if slot == 0 else edge_hi, row_slice]
            dst = buf.at[top if slot == 0 else 0, row_slice]
            return pltpu.make_async_remote_copy(
                src_ref=src, dst_ref=dst, send_sem=s_sem.at[slot, k], recv_sem=r_sem.at[slot, y],
                device_id=(z + (2 * slot - 1), k), device_id_type=MESH,
            )

        def to_peer(k):
            part = buf.at[own_layers, row_slice]
            return pltpu.make_async_remote_copy(
                src_ref=part, dst_ref=part, send_sem=s_sem.at[2, k], recv_sem=r_sem.at[2, y],
                device_id=(z, lax.rem(y + k, n_y)), device_id_type=MESH,
            )

        return to_side, to_peer

    def start_all(to_side, to_peer):
        for slot, has in ((0, has_lo), (1, has_hi)):
            @pl.when(has)
            def _():
                for k in range(n_y):
                    to_side(slot, k).start()
        for k in range(1, n_y):
            to_peer(k).start()

    def await_sends(to_side, to_peer):
        for slot, has in ((0, has_lo), (1, has_hi)):
            @pl.when(has)
            def _():
                for k in range(n_y):
                    to_side(slot, k).wait_send()
        for k in range(1, n_y):
            to_peer(k).wait_send()

    def recv(dst, sem, s_sem):
        pltpu.make_async_remote_copy(
            src_ref=dst, dst_ref=dst, send_sem=s_sem, recv_sem=sem, device_id=(z, y), device_id_type=MESH
        ).wait_recv()

    side_a, peer_a = send_lower(ga, 1, d2, pl.ds(1, d2), d2 + 1, mine, as_sem, ar_sem)
    start_all(side_a, peer_a)
    out_a[...] = full.astype(BF16)

    def tapped_b(first, count):
        rows = ga[first:first + count].astype(F32).reshape(count * hh * x2, ca)
        sb[first:first + count, 1:hh + 1] = tapped(rows, x2).astype(BF16).reshape(count, hh, x2, k3)

    def part_b(first, count, i):
        rows = jnp.concatenate([sb[first:first + count, j:j + hh].reshape(count * hh * x2, k3) for j in range(3)], axis=-1)
        return dot(rows, wb[i]).reshape(count, hh, x2, cb)

    loads[2].wait()
    for i in range(3):
        for tap in range(9):
            wb[i, tap * ca:(tap + 1) * ca] = wt[9 * i + tap].T
    for k in range(1, n_y):
        q = lax.rem(y + k, n_y)
        recv(ga.at[pl.ds(1, d2), pl.ds(q * h2, h2)], ar_sem.at[2, q], as_sem.at[2, k])
    tapped_b(1, d2)
    bias = jnp.broadcast_to(bb[...], (d2 * hh * x2, cb)).reshape(d2, hh, x2, cb)
    acc_b[...] = bias + part_b(1, d2, 1)
    acc_b[1:] += part_b(1, d2 - 1, 0)
    acc_b[:d2 - 1] += part_b(2, d2 - 1, 2)
    for slot, has, first, layer, i in ((1, has_lo, 0, 0, 0), (0, has_hi, d2 + 1, d2 - 1, 2)):
        @pl.when(has)
        def _():
            for k in range(n_y):
                recv(ga.at[first, pl.ds(k * h2, h2)], ar_sem.at[slot, k], as_sem.at[slot, k])
        tapped_b(first, 1)
        acc_b[layer] += part_b(first, 1, i)[0]

    full_b = jnp.maximum(acc_b[...], 0.0)
    paired = jnp.max(full_b.reshape(hh // 2, 2, x2, cb) if d2 == 1 else jnp.max(full_b, axis=0).reshape(h4, 2, x2, cb), axis=1)
    wide = []
    for q in range(per):
        parts = [jnp.where(lax.rem(y, per) == q, paired, 0.0) if p == q else jnp.zeros_like(paired) for p in range(per)]
        wide.append(jnp.concatenate(parts, axis=-1))
    pool_b[...] = functools.reduce(jnp.add, wide).reshape(h4 * x2, lanes)
    small = jnp.maximum(pool_b[pl.ds(0, h4 * x4, stride=2)], pool_b[pl.ds(1, h4 * x4, stride=2)])
    gb[1, pl.ds(y, 1)] = small.astype(BF16)[None]
    side_b, peer_b = send_lower(gb, 1, 1, 1, 2, pl.ds(y, 1), bs_sem, br_sem)
    start_all(side_b, peer_b)
    out_b[...] = full_b.astype(BF16)

    cells = h4 * x4

    def part_c(layer):
        groups = []
        for g in range(n_y // per):
            groups.append(functools.reduce(jnp.add, [gb[layer, g * per + p].astype(F32) for p in range(per)]))
        rows = jnp.concatenate(groups, axis=-1)
        sc[layer, 1:h4 + 1] = tapped(rows, x4).reshape(h4, x4, sc.shape[-1])
        lhs = jnp.concatenate([sc[layer, j:j + h4].reshape(cells, sc.shape[-1]) for j in range(3)], axis=-1)
        return dot(lhs.astype(BF16), wc[layer])

    loads[3].wait()
    for k in range(1, n_y):
        q = lax.rem(y + k, n_y)
        recv(gb.at[1, pl.ds(q, 1)], br_sem.at[2, q], bs_sem.at[2, k])
    total = bc[...] + part_c(1)
    for slot, has, layer in ((1, has_lo, 0), (0, has_hi, 2)):
        @pl.when(has)
        def _():
            for k in range(n_y):
                recv(gb.at[layer, pl.ds(k, 1)], br_sem.at[slot, k], bs_sem.at[slot, k])
    total += part_c(0) + part_c(2)
    out_c[...] = jnp.maximum(total, 0.0).astype(BF16)

    for index, (dz, dy) in enumerate(moves):
        @pl.when(inside(dz, dy))
        def _():
            halo(index, dz, dy).wait_send()
    await_sends(side_a, peer_a)
    await_sends(side_b, peer_b)


def put_out(*refs):
    sem = refs[-1]
    copies = [pltpu.make_async_copy(refs[i], refs[i + 3], sem.at[i]) for i in range(3)]
    for copy in copies:
        copy.start()
    for copy in copies:
        copy.wait()


def on_device(n_z, n_y, volume, kernel_a, bias_a, kernel_b, bias_b, kernel_c, bias_c):
    d, h, xw, ca = volume.shape
    cb, cc = kernel_b.shape[-1], kernel_c.shape[-1]
    c_in = kernel_c.shape[-2]
    d2, h2, x2 = d // 2, h // 2, xw // 2
    hh = h2 * n_y
    h4, x4 = hh // 2, x2 // 2
    lanes = 128
    wa = kernel_a.reshape(3, 3, 3 * ca, ca)
    wb = jnp.swapaxes(kernel_b, 3, 4).reshape(27, cb, ca)
    wc = kernel_c.reshape(3, 9 * c_in, cc)
    vmem = pl.BlockSpec(memory_space=pltpu.VMEM)
    hbm = pl.BlockSpec(memory_space=pl.ANY)
    shapes = ((d, h, xw, ca), (d2, hh, x2, cb), (h4 * x4, cc))
    results = pl.pallas_call(
        functools.partial(kernel, n_z, n_y),
        out_shape=tuple(pltpu.VMEM(shape, BF16) for shape in shapes),
        in_specs=[hbm, hbm, vmem, hbm, vmem, hbm, vmem],
        out_specs=(vmem, vmem, vmem),
        scratch_shapes=[
            pltpu.VMEM(volume.shape, BF16),
            pltpu.VMEM((2, h + 2, xw, ca), BF16),
            pltpu.VMEM((2, d, xw, ca), BF16),
            pltpu.VMEM(wa.shape, BF16),
            pltpu.VMEM(wb.shape, BF16),
            pltpu.VMEM((3, 9 * ca, cb), BF16),
            pltpu.VMEM(wc.shape, BF16),
            pltpu.VMEM((d, h, xw, 3 * ca), BF16),
            pltpu.VMEM((2, h + 2, xw, 3 * ca), BF16),
            pltpu.VMEM((2, d + 2, xw, 3 * ca), BF16),
            pltpu.VMEM((d, h, xw, ca), F32),
            pltpu.VMEM((d2 * h2 * xw, ca), F32),
            pltpu.VMEM((d2 + 2, hh, x2, ca), BF16),
            pltpu.VMEM((d2 + 2, hh + 2, x2, 3 * ca), BF16),
            pltpu.VMEM((d2, hh, x2, cb), F32),
            pltpu.VMEM((h4 * x2, lanes), F32),
            pltpu.VMEM((3, n_y, h4 * x4, lanes), BF16),
            pltpu.VMEM((3, h4 + 2, x4, 3 * c_in), F32),
            pltpu.SemaphoreType.DMA((4,)),
            pltpu.SemaphoreType.DMA((8,)),
            pltpu.SemaphoreType.DMA((8,)),
            pltpu.SemaphoreType.DMA((3, n_y)),
            pltpu.SemaphoreType.DMA((3, n_y)),
            pltpu.SemaphoreType.DMA((3, n_y)),
            pltpu.SemaphoreType.DMA((3, n_y)),
        ],
        compiler_params=pltpu.CompilerParams(collective_id=0, has_side_effects=True),
        name="unet",
    )(volume, wa, bias_a.reshape(1, -1), wb, bias_b.reshape(1, -1), wc, bias_c.reshape(1, -1))
    out_a, out_b, out_c = pl.pallas_call(
        put_out,
        out_shape=tuple(jax.ShapeDtypeStruct(shape, BF16) for shape in shapes),
        in_specs=[vmem] * 3,
        out_specs=(hbm,) * 3,
        scratch_shapes=[pltpu.SemaphoreType.DMA((3,))],
        name="put_out",
    )(*[pltpu.with_memory_space_constraint(r, pltpu.VMEM) for r in results])
    return out_a, out_b, out_c.reshape(d2 // 2, h4, x4, cc)


def solution(mesh):
    sizes = dict(mesh.shape)
    return jax.shard_map(
        functools.partial(on_device, sizes["gz"], sizes["gy"]),
        mesh=mesh,
        in_specs=(
            P("gz", "gy", None, None),
            P(),
            P(),
            P(None, None, None, None, "gy"),
            P("gy"),
            P(None, None, None, None, "gy"),
            P("gy"),
        ),
        out_specs=(P("gz", "gy", None, None), P("gz", None, None, "gy"), P("gz", None, None, "gy")),
        check_vma=False,
    )
```

```python
import functools

import jax
import jax.numpy as jnp
from jax import lax
from jax.experimental import pallas as pl
from jax.experimental.pallas import tpu as pltpu
from jax.sharding import PartitionSpec as P

F32 = jnp.float32
BF16 = jnp.bfloat16
MESH = pl.DeviceIdType.MESH


def tapped(rows, width):
    count = rows.shape[0]
    x = lax.broadcasted_iota(jnp.int32, rows.shape, 0) % width
    left = jnp.where(x == 0, 0.0, pltpu.roll(rows, 1, 0))
    right = jnp.where(x == width - 1, 0.0, pltpu.roll(rows, count - 1, 0))
    return jnp.concatenate([left, rows, right], axis=-1)


def dot(a, b):
    return jnp.dot(a, b, preferred_element_type=F32)


def kernel(
    n_z, n_y,
    vol, ka, bias_a, kb, bias_b, kc, bias_c,
    out_a, out_b, out_c,
    loc, hz, hy, wa, wt, wb, wc, ba, bb, bc,
    sa, sz, sy, acc_a, pool_a, ga, sb, acc_b, pool_b, gb, sc,
    perm, load_sem, hs_sem, hr_sem, as_sem, ar_sem, bs_sem, br_sem,
):
    z = lax.axis_index("gz")
    y = lax.axis_index("gy")
    d, h, xw, ca = vol.shape
    d2, h2, x2 = d // 2, h // 2, xw // 2
    hh = h2 * n_y
    cb = kb.shape[-2]
    h4, x4 = hh // 2, x2 // 2
    lanes = gb.shape[-1]
    per = lanes // cb

    loads = [
        pltpu.make_async_copy(vol, loc, load_sem.at[0]),
        pltpu.make_async_copy(ka, wa, load_sem.at[1]),
        pltpu.make_async_copy(kb, wt, load_sem.at[2]),
        pltpu.make_async_copy(kc, wc, load_sem.at[3]),
        pltpu.make_async_copy(bias_a, ba, load_sem.at[4]),
        pltpu.make_async_copy(bias_b, bb, load_sem.at[5]),
        pltpu.make_async_copy(bias_c, bc, load_sem.at[6]),
    ]

    has_lo, has_hi = z > 0, z < n_z - 1

    barrier = pltpu.get_barrier_semaphore()
    for away, has in ((-1, has_lo), (1, has_hi)):
        @pl.when(has)
        def _():
            pl.semaphore_signal(barrier, inc=1, device_id=(z + away, y), device_id_type=MESH)
    for k in range(1, n_y):
        pl.semaphore_signal(barrier, inc=1, device_id=(z, lax.rem(y + k, n_y)), device_id_type=MESH)
    for load in loads:
        load.start()
    sides = jnp.where(has_lo, 1, 0) + jnp.where(has_hi, 1, 0)

    def halo(index, dz, dy):
        layer = d - 1 if dz > 0 else 0
        row = h - 1 if dy > 0 else 0
        slot = 0 if dz > 0 else 1
        if dz == 0:
            src, dst = vol.at[:, row], hy.at[0 if dy > 0 else 1]
        elif dy == 0:
            src, dst = vol.at[layer], hz.at[slot, pl.ds(1, h)]
        else:
            src, dst = vol.at[layer, row], hz.at[slot, 0 if dy > 0 else h + 1]
        return pltpu.make_async_remote_copy(
            src_ref=src, dst_ref=dst, send_sem=hs_sem.at[index], recv_sem=hr_sem.at[index],
            device_id=(z + dz, y + dy), device_id_type=MESH,
        )

    def inside(dz, dy):
        ok = None
        for pos, count, step in ((z, n_z, dz), (y, n_y, dy)):
            if step:
                one = pos > 0 if step < 0 else pos < count - 1
                ok = one if ok is None else jnp.logical_and(ok, one)
        return ok

    moves = [(-1, 0), (1, 0), (-1, -1), (-1, 1), (1, -1), (1, 1), (0, -1), (0, 1)]
    pl.semaphore_wait(barrier, sides + n_y - 1)
    for slot, dy in ((0, 1), (1, -1)):
        @pl.when(inside(0, dy))
        def _():
            pl.semaphore_signal(perm.at[slot], inc=1, device_id=(z, y + dy), device_id_type=MESH)
    for index, (dz, dy) in enumerate(moves):
        if dz == 0 or dy == 0:
            @pl.when(inside(dz, dy))
            def _():
                halo(index, dz, dy).start()
    for slot, side in ((0, -1), (1, 1)):
        @pl.when(inside(0, side))
        def _():
            pl.semaphore_wait(perm.at[slot], 1)
            for index, (dz, dy) in enumerate(moves):
                if dz != 0 and dy == side:
                    @pl.when(inside(dz, 0))
                    def _():
                        halo(index, dz, dy).start()

    for slot, has in ((0, has_lo), (1, has_hi)):
        @pl.when(jnp.logical_not(has))
        def _():
            hz[slot] = jnp.zeros(hz.shape[1:], BF16)
            ga[slot * (d2 + 1)] = jnp.zeros(ga.shape[1:], BF16)
            gb[slot * 2] = jnp.zeros(gb.shape[1:], BF16)
    for slot, has_y, row in ((0, y > 0, 0), (1, y < n_y - 1, h + 1)):
        @pl.when(jnp.logical_not(has_y))
        def _():
            hy[slot] = jnp.zeros(hy.shape[1:], BF16)
            for s, has in ((0, has_lo), (1, has_hi)):
                @pl.when(has)
                def _():
                    hz[s, row] = jnp.zeros(hz.shape[2:], BF16)
    for row in (0, hh + 1):
        sb[:, row] = jnp.zeros((d2 + 2,) + sb.shape[2:], BF16)
    for row in (0, h4 + 1):
        sc[:, row] = jnp.zeros((3,) + sc.shape[2:], F32)
    for slot in (0, 1):
        for end in (0, d + 1):
            sy[slot, end] = jnp.zeros(sy.shape[2:], BF16)

    loads[0].wait()
    sa[...] = tapped(loc[...].astype(F32).reshape(d * h * xw, ca), xw).astype(BF16).reshape(sa.shape)
    loads[1].wait()
    loads[4].wait()
    k3 = 3 * ca

    def span(tap, count):
        low, high = max(0, 1 - tap), min(count, count + 1 - tap)
        return low, high, low + tap - 1, high + tap - 1

    bias = jnp.broadcast_to(ba[...], (d * h * xw, ca)).reshape(d, h, xw, ca)
    acc_a[...] = bias + dot(sa[...].reshape(d * h * xw, k3), wa[1, 1]).reshape(d, h, xw, ca)
    for i in range(3):
        for j in range(3):
            if (i, j) == (1, 1):
                continue
            z0, z1, f0, f1 = span(i, d)
            y0, y1, g0, g1 = span(j, h)
            rows = sa[f0:f1, g0:g1].reshape(-1, k3)
            acc_a[z0:z1, y0:y1] += dot(rows, wa[i, j]).reshape(z1 - z0, y1 - y0, xw, ca)

    for index, (dz, dy) in enumerate(moves):
        if dz == 0:
            @pl.when(inside(-dz, -dy))
            def _():
                halo(index, dz, dy).wait_recv()
    for slot, row, tap in ((0, 0, 0), (1, h - 1, 2)):
        sy[slot, 1:d + 1] = tapped(hy[slot].astype(F32).reshape(d * xw, ca), xw).astype(BF16).reshape(d, xw, k3)
        total = acc_a[:, row].reshape(d * xw, ca)
        for i in range(3):
            total += dot(sy[slot, i:i + d].reshape(d * xw, k3), wa[i, tap])
        acc_a[:, row] = total.reshape(d, xw, ca)
    for index, (dz, dy) in enumerate(moves):
        if dz != 0:
            @pl.when(inside(-dz, -dy))
            def _():
                halo(index, dz, dy).wait_recv()
    for slot, layer, tap in ((0, 0, 0), (1, d - 1, 2)):
        sz[slot] = tapped(hz[slot].astype(F32).reshape((h + 2) * xw, ca), xw).astype(BF16).reshape(h + 2, xw, k3)
        total = acc_a[layer].reshape(h * xw, ca)
        for j in range(3):
            total += dot(sz[slot, j:j + h].reshape(h * xw, k3), wa[tap, j])
        acc_a[layer] = total.reshape(h, xw, ca)

    full = jnp.maximum(acc_a[...], 0.0)
    paired = jnp.max(full.reshape(d2, 2, h2, 2, xw, ca), axis=(1, 3))
    pool_a[...] = paired.reshape(d2 * h2 * xw, ca)
    half = d2 * h2 * x2
    small = jnp.maximum(pool_a[pl.ds(0, half, stride=2)], pool_a[pl.ds(1, half, stride=2)])
    mine = pl.ds(y * h2, h2)
    ga[1:d2 + 1, mine] = small.astype(BF16).reshape(d2, h2, x2, ca)

    def send_lower(buf, edge_lo, edge_hi, own_layers, top, row_slice, s_sem, r_sem):
        def to_side(slot, k):
            src = buf.at[edge_lo if slot == 0 else edge_hi, row_slice]
            dst = buf.at[top if slot == 0 else 0, row_slice]
            return pltpu.make_async_remote_copy(
                src_ref=src, dst_ref=dst, send_sem=s_sem.at[slot, k], recv_sem=r_sem.at[slot, y],
                device_id=(z + (2 * slot - 1), k), device_id_type=MESH,
            )

        def to_peer(k):
            part = buf.at[own_layers, row_slice]
            return pltpu.make_async_remote_copy(
                src_ref=part, dst_ref=part, send_sem=s_sem.at[2, k], recv_sem=r_sem.at[2, y],
                device_id=(z, lax.rem(y + k, n_y)), device_id_type=MESH,
            )

        return to_side, to_peer

    def start_all(to_side, to_peer):
        for slot, has in ((0, has_lo), (1, has_hi)):
            @pl.when(has)
            def _():
                for k in range(n_y):
                    to_side(slot, k).start()
        for k in range(1, n_y):
            to_peer(k).start()

    def await_sends(to_side, to_peer):
        for slot, has in ((0, has_lo), (1, has_hi)):
            @pl.when(has)
            def _():
                for k in range(n_y):
                    to_side(slot, k).wait_send()
        for k in range(1, n_y):
            to_peer(k).wait_send()

    def recv(dst, sem, s_sem):
        pltpu.make_async_remote_copy(
            src_ref=dst, dst_ref=dst, send_sem=s_sem, recv_sem=sem, device_id=(z, y), device_id_type=MESH
        ).wait_recv()

    side_a, peer_a = send_lower(ga, 1, d2, pl.ds(1, d2), d2 + 1, mine, as_sem, ar_sem)
    start_all(side_a, peer_a)
    out_a[...] = full.astype(BF16)

    def tapped_b(first, count):
        rows = ga[first:first + count].astype(F32).reshape(count * hh * x2, ca)
        sb[first:first + count, 1:hh + 1] = tapped(rows, x2).astype(BF16).reshape(count, hh, x2, k3)

    def part_b(first, count, i):
        rows = jnp.concatenate([sb[first:first + count, j:j + hh].reshape(count * hh * x2, k3) for j in range(3)], axis=-1)
        return dot(rows, wb[i]).reshape(count, hh, x2, cb)

    loads[2].wait()
    loads[5].wait()
    for i in range(3):
        for tap in range(9):
            wb[i, tap * ca:(tap + 1) * ca] = wt[9 * i + tap].T
    for k in range(1, n_y):
        q = lax.rem(y + k, n_y)
        recv(ga.at[pl.ds(1, d2), pl.ds(q * h2, h2)], ar_sem.at[2, q], as_sem.at[2, k])
    tapped_b(1, d2)
    bias = jnp.broadcast_to(bb[...], (d2 * hh * x2, cb)).reshape(d2, hh, x2, cb)
    acc_b[...] = bias + part_b(1, d2, 1)
    acc_b[1:] += part_b(1, d2 - 1, 0)
    acc_b[:d2 - 1] += part_b(2, d2 - 1, 2)
    for slot, has, first, layer, i in ((1, has_lo, 0, 0, 0), (0, has_hi, d2 + 1, d2 - 1, 2)):
        @pl.when(has)
        def _():
            for k in range(n_y):
                recv(ga.at[first, pl.ds(k * h2, h2)], ar_sem.at[slot, k], as_sem.at[slot, k])
        tapped_b(first, 1)
        acc_b[layer] += part_b(first, 1, i)[0]

    full_b = jnp.maximum(acc_b[...], 0.0)
    paired = jnp.max(full_b.reshape(hh // 2, 2, x2, cb) if d2 == 1 else jnp.max(full_b, axis=0).reshape(h4, 2, x2, cb), axis=1)
    wide = []
    for q in range(per):
        parts = [jnp.where(lax.rem(y, per) == q, paired, 0.0) if p == q else jnp.zeros_like(paired) for p in range(per)]
        wide.append(jnp.concatenate(parts, axis=-1))
    pool_b[...] = functools.reduce(jnp.add, wide).reshape(h4 * x2, lanes)
    small = jnp.maximum(pool_b[pl.ds(0, h4 * x4, stride=2)], pool_b[pl.ds(1, h4 * x4, stride=2)])
    gb[1, pl.ds(y, 1)] = small.astype(BF16)[None]
    side_b, peer_b = send_lower(gb, 1, 1, 1, 2, pl.ds(y, 1), bs_sem, br_sem)
    start_all(side_b, peer_b)
    out_b[...] = full_b.astype(BF16)

    cells = h4 * x4

    def part_c(layer):
        groups = []
        for g in range(n_y // per):
            groups.append(functools.reduce(jnp.add, [gb[layer, g * per + p].astype(F32) for p in range(per)]))
        rows = jnp.concatenate(groups, axis=-1)
        sc[layer, 1:h4 + 1] = tapped(rows, x4).reshape(h4, x4, sc.shape[-1])
        lhs = jnp.concatenate([sc[layer, j:j + h4].reshape(cells, sc.shape[-1]) for j in range(3)], axis=-1)
        return dot(lhs.astype(BF16), wc[layer])

    loads[3].wait()
    loads[6].wait()
    for k in range(1, n_y):
        q = lax.rem(y + k, n_y)
        recv(gb.at[1, pl.ds(q, 1)], br_sem.at[2, q], bs_sem.at[2, k])
    total = bc[...] + part_c(1)
    for slot, has, layer in ((1, has_lo, 0), (0, has_hi, 2)):
        @pl.when(has)
        def _():
            for k in range(n_y):
                recv(gb.at[layer, pl.ds(k, 1)], br_sem.at[slot, k], bs_sem.at[slot, k])
    total += part_c(0) + part_c(2)
    out_c[...] = jnp.maximum(total, 0.0).astype(BF16)

    for index, (dz, dy) in enumerate(moves):
        @pl.when(inside(dz, dy))
        def _():
            halo(index, dz, dy).wait_send()
    await_sends(side_a, peer_a)
    await_sends(side_b, peer_b)


def put_out(*refs):
    sem = refs[-1]
    copies = [pltpu.make_async_copy(refs[i], refs[i + 3], sem.at[i]) for i in range(3)]
    for copy in copies:
        copy.start()
    for copy in copies:
        copy.wait()


def on_device(n_z, n_y, volume, kernel_a, bias_a, kernel_b, bias_b, kernel_c, bias_c):
    d, h, xw, ca = volume.shape
    cb, cc = kernel_b.shape[-1], kernel_c.shape[-1]
    c_in = kernel_c.shape[-2]
    d2, h2, x2 = d // 2, h // 2, xw // 2
    hh = h2 * n_y
    h4, x4 = hh // 2, x2 // 2
    lanes = 128
    wa = kernel_a.reshape(3, 3, 3 * ca, ca)
    wb = jnp.swapaxes(kernel_b, 3, 4).reshape(27, cb, ca)
    wc = kernel_c.reshape(3, 9 * c_in, cc)
    vmem = pl.BlockSpec(memory_space=pltpu.VMEM)
    hbm = pl.BlockSpec(memory_space=pl.ANY)
    shapes = ((d, h, xw, ca), (d2, hh, x2, cb), (h4 * x4, cc))
    results = pl.pallas_call(
        functools.partial(kernel, n_z, n_y),
        out_shape=tuple(pltpu.VMEM(shape, BF16) for shape in shapes),
        in_specs=[hbm] * 7,
        out_specs=(vmem, vmem, vmem),
        scratch_shapes=[
            pltpu.VMEM(volume.shape, BF16),
            pltpu.VMEM((2, h + 2, xw, ca), BF16),
            pltpu.VMEM((2, d, xw, ca), BF16),
            pltpu.VMEM(wa.shape, BF16),
            pltpu.VMEM(wb.shape, BF16),
            pltpu.VMEM((3, 9 * ca, cb), BF16),
            pltpu.VMEM(wc.shape, BF16),
            pltpu.VMEM((1, ca), F32),
            pltpu.VMEM((1, cb), F32),
            pltpu.VMEM((1, cc), F32),
            pltpu.VMEM((d, h, xw, 3 * ca), BF16),
            pltpu.VMEM((2, h + 2, xw, 3 * ca), BF16),
            pltpu.VMEM((2, d + 2, xw, 3 * ca), BF16),
            pltpu.VMEM((d, h, xw, ca), F32),
            pltpu.VMEM((d2 * h2 * xw, ca), F32),
            pltpu.VMEM((d2 + 2, hh, x2, ca), BF16),
            pltpu.VMEM((d2 + 2, hh + 2, x2, 3 * ca), BF16),
            pltpu.VMEM((d2, hh, x2, cb), F32),
            pltpu.VMEM((h4 * x2, lanes), F32),
            pltpu.VMEM((3, n_y, h4 * x4, lanes), BF16),
            pltpu.VMEM((3, h4 + 2, x4, 3 * c_in), F32),
            pltpu.SemaphoreType.REGULAR((2,)),
            pltpu.SemaphoreType.DMA((7,)),
            pltpu.SemaphoreType.DMA((8,)),
            pltpu.SemaphoreType.DMA((8,)),
            pltpu.SemaphoreType.DMA((3, n_y)),
            pltpu.SemaphoreType.DMA((3, n_y)),
            pltpu.SemaphoreType.DMA((3, n_y)),
            pltpu.SemaphoreType.DMA((3, n_y)),
        ],
        compiler_params=pltpu.CompilerParams(collective_id=0, has_side_effects=True),
        name="unet",
    )(volume, wa, bias_a.reshape(1, -1), wb, bias_b.reshape(1, -1), wc, bias_c.reshape(1, -1))
    out_a, out_b, out_c = pl.pallas_call(
        put_out,
        out_shape=tuple(jax.ShapeDtypeStruct(shape, BF16) for shape in shapes),
        in_specs=[vmem] * 3,
        out_specs=(hbm,) * 3,
        scratch_shapes=[pltpu.SemaphoreType.DMA((3,))],
        name="put_out",
    )(*[pltpu.with_memory_space_constraint(r, pltpu.VMEM) for r in results])
    return out_a, out_b, out_c.reshape(d2 // 2, h4, x4, cc)


def solution(mesh):
    sizes = dict(mesh.shape)
    return jax.shard_map(
        functools.partial(on_device, sizes["gz"], sizes["gy"]),
        mesh=mesh,
        in_specs=(
            P("gz", "gy", None, None),
            P(),
            P(),
            P(None, None, None, None, "gy"),
            P("gy"),
            P(None, None, None, None, "gy"),
            P("gy"),
        ),
        out_specs=(P("gz", "gy", None, None), P("gz", None, None, "gy"), P("gz", None, None, "gy")),
        check_vma=False,
    )
```

```python
import functools

import jax
import jax.numpy as jnp
from jax import lax
from jax.experimental import pallas as pl
from jax.experimental.pallas import tpu as pltpu
from jax.sharding import PartitionSpec as P

F32 = jnp.float32
BF16 = jnp.bfloat16
MESH = pl.DeviceIdType.MESH


def tapped(rows, width):
    count = rows.shape[0]
    x = lax.broadcasted_iota(jnp.int32, rows.shape, 0) % width
    left = jnp.where(x == 0, 0.0, pltpu.roll(rows, 1, 0))
    right = jnp.where(x == width - 1, 0.0, pltpu.roll(rows, count - 1, 0))
    return jnp.concatenate([left, rows, right], axis=-1)


def dot(a, b):
    return jnp.dot(a, b, preferred_element_type=F32)


def kernel(
    n_z, n_y,
    vol, ka, bias_a, kb, bias_b, kc, bias_c,
    out_a, out_b, out_c,
    loc, hz, hy, wa, wt, wb, wc, ba, bb, bc,
    sa, sz, sy, acc_a, pool_a, ga, sb, acc_b, pool_b, gb, sc,
    perm, load_sem, hs_sem, hr_sem, as_sem, ar_sem, bs_sem, br_sem,
):
    z = lax.axis_index("gz")
    y = lax.axis_index("gy")
    d, h, xw, ca = vol.shape
    d2, h2, x2 = d // 2, h // 2, xw // 2
    hh = h2 * n_y
    cb = kb.shape[-2]
    h4, x4 = hh // 2, x2 // 2
    lanes = gb.shape[-1]
    per = lanes // cb

    loads = [
        pltpu.make_async_copy(vol, loc, load_sem.at[0]),
        pltpu.make_async_copy(ka, wa, load_sem.at[1]),
        pltpu.make_async_copy(kb, wt, load_sem.at[2]),
        pltpu.make_async_copy(kc, wc, load_sem.at[3]),
        pltpu.make_async_copy(bias_a, ba, load_sem.at[4]),
        pltpu.make_async_copy(bias_b, bb, load_sem.at[5]),
        pltpu.make_async_copy(bias_c, bc, load_sem.at[6]),
    ]

    has_lo, has_hi = z > 0, z < n_z - 1

    barrier = pltpu.get_barrier_semaphore()
    for away, has in ((-1, has_lo), (1, has_hi)):
        @pl.when(has)
        def _():
            pl.semaphore_signal(barrier, inc=1, device_id=(z + away, y), device_id_type=MESH)
    for k in range(1, n_y):
        pl.semaphore_signal(barrier, inc=1, device_id=(z, lax.rem(y + k, n_y)), device_id_type=MESH)
    for load in loads:
        load.start()
    sides = jnp.where(has_lo, 1, 0) + jnp.where(has_hi, 1, 0)

    def halo(index, dz, dy):
        layer = d - 1 if dz > 0 else 0
        row = h - 1 if dy > 0 else 0
        slot = 0 if dz > 0 else 1
        if dz == 0:
            src, dst = vol.at[:, row], hy.at[0 if dy > 0 else 1]
        elif dy == 0:
            src, dst = vol.at[layer], hz.at[slot, pl.ds(1, h)]
        else:
            src, dst = vol.at[layer, row], hz.at[slot, 0 if dy > 0 else h + 1]
        return pltpu.make_async_remote_copy(
            src_ref=src, dst_ref=dst, send_sem=hs_sem.at[index], recv_sem=hr_sem.at[index],
            device_id=(z + dz, y + dy), device_id_type=MESH,
        )

    def inside(dz, dy):
        ok = None
        for pos, count, step in ((z, n_z, dz), (y, n_y, dy)):
            if step:
                one = pos > 0 if step < 0 else pos < count - 1
                ok = one if ok is None else jnp.logical_and(ok, one)
        return ok

    moves = [(-1, 0), (1, 0), (-1, -1), (-1, 1), (1, -1), (1, 1), (0, -1), (0, 1)]
    pl.semaphore_wait(barrier, sides + n_y - 1)
    for slot, dy in ((0, 1), (1, -1)):
        @pl.when(inside(0, dy))
        def _():
            pl.semaphore_signal(perm.at[slot], inc=1, device_id=(z, y + dy), device_id_type=MESH)
    for index, (dz, dy) in enumerate(moves):
        if dz == 0 or dy == 0:
            @pl.when(inside(dz, dy))
            def _():
                halo(index, dz, dy).start()
    for slot, side in ((0, -1), (1, 1)):
        @pl.when(inside(0, side))
        def _():
            pl.semaphore_wait(perm.at[slot], 1)
            for index, (dz, dy) in enumerate(moves):
                if dz != 0 and dy == side:
                    @pl.when(inside(dz, 0))
                    def _():
                        halo(index, dz, dy).start()

    for slot, has in ((0, has_lo), (1, has_hi)):
        @pl.when(jnp.logical_not(has))
        def _():
            hz[slot] = jnp.zeros(hz.shape[1:], BF16)
            ga[slot * (d2 + 1)] = jnp.zeros(ga.shape[1:], BF16)
            gb[slot * 2] = jnp.zeros(gb.shape[1:], BF16)
    for slot, has_y, row in ((0, y > 0, 0), (1, y < n_y - 1, h + 1)):
        @pl.when(jnp.logical_not(has_y))
        def _():
            hy[slot] = jnp.zeros(hy.shape[1:], BF16)
            for s, has in ((0, has_lo), (1, has_hi)):
                @pl.when(has)
                def _():
                    hz[s, row] = jnp.zeros(hz.shape[2:], BF16)
    for row in (0, hh + 1):
        sb[:, row] = jnp.zeros((d2 + 2,) + sb.shape[2:], BF16)
    for row in (0, h4 + 1):
        sc[:, row] = jnp.zeros((3,) + sc.shape[2:], F32)
    for slot in (0, 1):
        for end in (0, d + 1):
            sy[slot, end] = jnp.zeros(sy.shape[2:], BF16)

    loads[0].wait()
    sa[...] = tapped(loc[...].astype(F32).reshape(d * h * xw, ca), xw).astype(BF16).reshape(sa.shape)
    loads[1].wait()
    loads[4].wait()
    k3 = 3 * ca

    def span(tap, count):
        low, high = max(0, 1 - tap), min(count, count + 1 - tap)
        return low, high, low + tap - 1, high + tap - 1

    bias = jnp.broadcast_to(ba[...], (d * h * xw, ca)).reshape(d, h, xw, ca)
    acc_a[...] = bias + dot(sa[...].reshape(d * h * xw, k3), wa[1, 1]).reshape(d, h, xw, ca)
    for i in range(3):
        for j in range(3):
            if (i, j) == (1, 1):
                continue
            z0, z1, f0, f1 = span(i, d)
            y0, y1, g0, g1 = span(j, h)
            rows = sa[f0:f1, g0:g1].reshape(-1, k3)
            acc_a[z0:z1, y0:y1] += dot(rows, wa[i, j]).reshape(z1 - z0, y1 - y0, xw, ca)

    for index, (dz, dy) in enumerate(moves):
        if dz == 0:
            @pl.when(inside(-dz, -dy))
            def _():
                halo(index, dz, dy).wait_recv()
    for slot, row, tap in ((0, 0, 0), (1, h - 1, 2)):
        sy[slot, 1:d + 1] = tapped(hy[slot].astype(F32).reshape(d * xw, ca), xw).astype(BF16).reshape(d, xw, k3)
        total = acc_a[:, row].reshape(d * xw, ca)
        for i in range(3):
            total += dot(sy[slot, i:i + d].reshape(d * xw, k3), wa[i, tap])
        acc_a[:, row] = total.reshape(d, xw, ca)
    mine = pl.ds(y * h2, h2)

    def send_lower(buf, edge_lo, edge_hi, own_layers, top, row_slice, s_sem, r_sem):
        def to_side(slot, k):
            src = buf.at[edge_lo if slot == 0 else edge_hi, row_slice]
            dst = buf.at[top if slot == 0 else 0, row_slice]
            return pltpu.make_async_remote_copy(
                src_ref=src, dst_ref=dst, send_sem=s_sem.at[slot, k], recv_sem=r_sem.at[slot, y],
                device_id=(z + (2 * slot - 1), k), device_id_type=MESH,
            )

        def to_peer(k):
            part = buf.at[own_layers, row_slice]
            return pltpu.make_async_remote_copy(
                src_ref=part, dst_ref=part, send_sem=s_sem.at[2, k], recv_sem=r_sem.at[2, y],
                device_id=(z, lax.rem(y + k, n_y)), device_id_type=MESH,
            )

        return to_side, to_peer

    def start_all(to_side, to_peer):
        for slot, has in ((0, has_lo), (1, has_hi)):
            @pl.when(has)
            def _():
                for k in range(n_y):
                    to_side(slot, k).start()
        for k in range(1, n_y):
            to_peer(k).start()

    def await_sends(to_side, to_peer):
        for slot, has in ((0, has_lo), (1, has_hi)):
            @pl.when(has)
            def _():
                for k in range(n_y):
                    to_side(slot, k).wait_send()
        for k in range(1, n_y):
            to_peer(k).wait_send()

    def recv(dst, sem, s_sem):
        pltpu.make_async_remote_copy(
            src_ref=dst, dst_ref=dst, send_sem=s_sem, recv_sem=sem, device_id=(z, y), device_id_type=MESH
        ).wait_recv()

    side_a, peer_a = send_lower(ga, 1, d2, pl.ds(1, d2), d2 + 1, mine, as_sem, ar_sem)

    def pool_layer(p):
        pair = jnp.maximum(acc_a[2 * p:2 * p + 2], 0.0)
        pool_a[pl.ds(p * h2 * xw, h2 * xw)] = jnp.max(pair.reshape(2, h2, 2, xw, ca), axis=(0, 2)).reshape(h2 * xw, ca)
        even, odd = (pool_a[pl.ds(p * h2 * xw + q, h2 * x2, stride=2)] for q in (0, 1))
        ga[1 + p, mine] = jnp.maximum(even, odd).astype(BF16).reshape(h2, x2, ca)

    for p in range(1, d2 - 1):
        pool_layer(p)
    for slot, layer, tap, has in ((0, 0, 0, has_lo), (1, d - 1, 2, has_hi)):
        for index, (dz, dy) in enumerate(moves):
            if dz == 1 - 2 * slot:
                @pl.when(inside(-dz, -dy))
                def _():
                    halo(index, dz, dy).wait_recv()
        sz[slot] = tapped(hz[slot].astype(F32).reshape((h + 2) * xw, ca), xw).astype(BF16).reshape(h + 2, xw, k3)
        total = acc_a[layer].reshape(h * xw, ca)
        for j in range(3):
            total += dot(sz[slot, j:j + h].reshape(h * xw, k3), wa[tap, j])
        acc_a[layer] = total.reshape(h, xw, ca)
        pool_layer(slot * (d2 - 1))
        @pl.when(has)
        def _():
            for k in range(n_y):
                side_a(slot, k).start()
    for k in range(1, n_y):
        peer_a(k).start()
    out_a[...] = jnp.maximum(acc_a[...], 0.0).astype(BF16)

    def tapped_b(first, count):
        rows = ga[first:first + count].astype(F32).reshape(count * hh * x2, ca)
        sb[first:first + count, 1:hh + 1] = tapped(rows, x2).astype(BF16).reshape(count, hh, x2, k3)

    def part_b(first, count, i):
        rows = jnp.concatenate([sb[first:first + count, j:j + hh].reshape(count * hh * x2, k3) for j in range(3)], axis=-1)
        return dot(rows, wb[i]).reshape(count, hh, x2, cb)

    loads[2].wait()
    loads[5].wait()
    for i in range(3):
        for tap in range(9):
            wb[i, tap * ca:(tap + 1) * ca] = wt[9 * i + tap].T
    for k in range(1, n_y):
        q = lax.rem(y + k, n_y)
        recv(ga.at[pl.ds(1, d2), pl.ds(q * h2, h2)], ar_sem.at[2, q], as_sem.at[2, k])
    tapped_b(1, d2)
    bias = jnp.broadcast_to(bb[...], (d2 * hh * x2, cb)).reshape(d2, hh, x2, cb)
    acc_b[...] = bias + part_b(1, d2, 1)
    acc_b[1:] += part_b(1, d2 - 1, 0)
    acc_b[:d2 - 1] += part_b(2, d2 - 1, 2)
    for slot, has, first, layer, i in ((1, has_lo, 0, 0, 0), (0, has_hi, d2 + 1, d2 - 1, 2)):
        @pl.when(has)
        def _():
            for k in range(n_y):
                recv(ga.at[first, pl.ds(k * h2, h2)], ar_sem.at[slot, k], as_sem.at[slot, k])
        tapped_b(first, 1)
        acc_b[layer] += part_b(first, 1, i)[0]

    full_b = jnp.maximum(acc_b[...], 0.0)
    paired = jnp.max(full_b.reshape(hh // 2, 2, x2, cb) if d2 == 1 else jnp.max(full_b, axis=0).reshape(h4, 2, x2, cb), axis=1)
    wide = []
    for q in range(per):
        parts = [jnp.where(lax.rem(y, per) == q, paired, 0.0) if p == q else jnp.zeros_like(paired) for p in range(per)]
        wide.append(jnp.concatenate(parts, axis=-1))
    pool_b[...] = functools.reduce(jnp.add, wide).reshape(h4 * x2, lanes)
    small = jnp.maximum(pool_b[pl.ds(0, h4 * x4, stride=2)], pool_b[pl.ds(1, h4 * x4, stride=2)])
    gb[1, pl.ds(y, 1)] = small.astype(BF16)[None]
    side_b, peer_b = send_lower(gb, 1, 1, 1, 2, pl.ds(y, 1), bs_sem, br_sem)
    start_all(side_b, peer_b)
    out_b[...] = full_b.astype(BF16)

    cells = h4 * x4

    def part_c(layer):
        groups = []
        for g in range(n_y // per):
            groups.append(functools.reduce(jnp.add, [gb[layer, g * per + p].astype(F32) for p in range(per)]))
        rows = jnp.concatenate(groups, axis=-1)
        sc[layer, 1:h4 + 1] = tapped(rows, x4).reshape(h4, x4, sc.shape[-1])
        lhs = jnp.concatenate([sc[layer, j:j + h4].reshape(cells, sc.shape[-1]) for j in range(3)], axis=-1)
        return dot(lhs.astype(BF16), wc[layer])

    loads[3].wait()
    loads[6].wait()
    for k in range(1, n_y):
        q = lax.rem(y + k, n_y)
        recv(gb.at[1, pl.ds(q, 1)], br_sem.at[2, q], bs_sem.at[2, k])
    total = bc[...] + part_c(1)
    for slot, has, layer in ((1, has_lo, 0), (0, has_hi, 2)):
        @pl.when(has)
        def _():
            for k in range(n_y):
                recv(gb.at[layer, pl.ds(k, 1)], br_sem.at[slot, k], bs_sem.at[slot, k])
    total += part_c(0) + part_c(2)
    out_c[...] = jnp.maximum(total, 0.0).astype(BF16)

    for index, (dz, dy) in enumerate(moves):
        @pl.when(inside(dz, dy))
        def _():
            halo(index, dz, dy).wait_send()
    await_sends(side_a, peer_a)
    await_sends(side_b, peer_b)


def put_out(*refs):
    sem = refs[-1]
    copies = [pltpu.make_async_copy(refs[i], refs[i + 3], sem.at[i]) for i in range(3)]
    for copy in copies:
        copy.start()
    for copy in copies:
        copy.wait()


def on_device(n_z, n_y, volume, kernel_a, bias_a, kernel_b, bias_b, kernel_c, bias_c):
    d, h, xw, ca = volume.shape
    cb, cc = kernel_b.shape[-1], kernel_c.shape[-1]
    c_in = kernel_c.shape[-2]
    d2, h2, x2 = d // 2, h // 2, xw // 2
    hh = h2 * n_y
    h4, x4 = hh // 2, x2 // 2
    lanes = 128
    wa = kernel_a.reshape(3, 3, 3 * ca, ca)
    wb = jnp.swapaxes(kernel_b, 3, 4).reshape(27, cb, ca)
    wc = kernel_c.reshape(3, 9 * c_in, cc)
    vmem = pl.BlockSpec(memory_space=pltpu.VMEM)
    hbm = pl.BlockSpec(memory_space=pl.ANY)
    shapes = ((d, h, xw, ca), (d2, hh, x2, cb), (h4 * x4, cc))
    results = pl.pallas_call(
        functools.partial(kernel, n_z, n_y),
        out_shape=tuple(pltpu.VMEM(shape, BF16) for shape in shapes),
        in_specs=[hbm] * 7,
        out_specs=(vmem, vmem, vmem),
        scratch_shapes=[
            pltpu.VMEM(volume.shape, BF16),
            pltpu.VMEM((2, h + 2, xw, ca), BF16),
            pltpu.VMEM((2, d, xw, ca), BF16),
            pltpu.VMEM(wa.shape, BF16),
            pltpu.VMEM(wb.shape, BF16),
            pltpu.VMEM((3, 9 * ca, cb), BF16),
            pltpu.VMEM(wc.shape, BF16),
            pltpu.VMEM((1, ca), F32),
            pltpu.VMEM((1, cb), F32),
            pltpu.VMEM((1, cc), F32),
            pltpu.VMEM((d, h, xw, 3 * ca), BF16),
            pltpu.VMEM((2, h + 2, xw, 3 * ca), BF16),
            pltpu.VMEM((2, d + 2, xw, 3 * ca), BF16),
            pltpu.VMEM((d, h, xw, ca), F32),
            pltpu.VMEM((d2 * h2 * xw, ca), F32),
            pltpu.VMEM((d2 + 2, hh, x2, ca), BF16),
            pltpu.VMEM((d2 + 2, hh + 2, x2, 3 * ca), BF16),
            pltpu.VMEM((d2, hh, x2, cb), F32),
            pltpu.VMEM((h4 * x2, lanes), F32),
            pltpu.VMEM((3, n_y, h4 * x4, lanes), BF16),
            pltpu.VMEM((3, h4 + 2, x4, 3 * c_in), F32),
            pltpu.SemaphoreType.REGULAR((2,)),
            pltpu.SemaphoreType.DMA((7,)),
            pltpu.SemaphoreType.DMA((8,)),
            pltpu.SemaphoreType.DMA((8,)),
            pltpu.SemaphoreType.DMA((3, n_y)),
            pltpu.SemaphoreType.DMA((3, n_y)),
            pltpu.SemaphoreType.DMA((3, n_y)),
            pltpu.SemaphoreType.DMA((3, n_y)),
        ],
        compiler_params=pltpu.CompilerParams(collective_id=0, has_side_effects=True),
        name="unet",
    )(volume, wa, bias_a.reshape(1, -1), wb, bias_b.reshape(1, -1), wc, bias_c.reshape(1, -1))
    out_a, out_b, out_c = pl.pallas_call(
        put_out,
        out_shape=tuple(jax.ShapeDtypeStruct(shape, BF16) for shape in shapes),
        in_specs=[vmem] * 3,
        out_specs=(hbm,) * 3,
        scratch_shapes=[pltpu.SemaphoreType.DMA((3,))],
        name="put_out",
    )(*[pltpu.with_memory_space_constraint(r, pltpu.VMEM) for r in results])
    return out_a, out_b, out_c.reshape(d2 // 2, h4, x4, cc)


def solution(mesh):
    sizes = dict(mesh.shape)
    return jax.shard_map(
        functools.partial(on_device, sizes["gz"], sizes["gy"]),
        mesh=mesh,
        in_specs=(
            P("gz", "gy", None, None),
            P(),
            P(),
            P(None, None, None, None, "gy"),
            P("gy"),
            P(None, None, None, None, "gy"),
            P("gy"),
        ),
        out_specs=(P("gz", "gy", None, None), P("gz", None, None, "gy"), P("gz", None, None, "gy")),
        check_vma=False,
    )
```
